32 devices in a mesh: pul: 4 (over y, x), rng: 8 (over z, core).
Axes of the slice: x: 2, y: 2, z: 4, core: 2. Of those that a mesh axis runs over, the one named last changes fastest.
Arguments:
- raw: bfloat16 [2, 2, 2048, 4096], P(None, None, 'pul', 'rng'), may hold values from -6 to 6
- range_chirp: bfloat16 [2, 256], replicated, may hold values from -0.25 to 0.25
- mig_weight: bfloat16 [2, 8, 4096], P(None, None, 'rng'), may hold values from -1.5 to 1.5
- mig_offset: int32 [4096], P('rng'), may hold values from 0 to 120, as said below
- aperture: int32 [4096], P('rng'), may hold values from 1 to 8, as said below
- az_rate: float32 [4096], P('rng'), may hold values from 0.25 to 1
Outputs:
- image: bfloat16 [2, 2, 4096, 2048], P(None, None, 'rng', 'pul')
The draws below stay inside these ranges and needn't reach their ends.
Inputs may be any that keep to these rules, and one draw needn't show every extreme that they name: `mig_offset`: one range bin and another are drawn at offsets 0 and 120; the other offsets are independent. The aperture of range bin r is min(8, 1 + floor(8 r / 4096) + j), with j 0 or 1 drawn for each bin and j = 0 at r = 0.
All inputs are finite; a program needn't handle non-finite values.
Results may differ from the reference program's by a relative error of at most 0.0064.
Values may be sent and summed in bfloat16 or wider, within the bound.
No kernel may reach another device: no remote copies, remote signals or barrier semaphores. Data moves between devices by JAX's collectives and lax.ppermute only.
A program may use at most 64 MiB of HBM per device.

```python
import math
import jax
import jax.numpy as jnp
from jax import lax

POL = 2
LR = 256
BW = 8
OFFMAX = 120
KMAX = 8
NA = 2048
NR = 4096


def draw_mig_offset(key, part):
    first_key, second_key, third_key = jax.random.split(jax.random.fold_in(key, 11), 3)
    offsets = jax.random.randint(first_key, (NR,), 0, OFFMAX + 1)
    high_pos = jax.random.randint(second_key, (), 0, NR)
    low_pos = jax.random.randint(third_key, (), 0, NR)
    range_index = jnp.arange(NR)
    offsets = jnp.where(range_index == low_pos, 0, offsets)
    offsets = jnp.where(range_index == high_pos, OFFMAX, offsets)
    return offsets.astype(jnp.int32)


def draw_aperture(key, part):
    range_index = jnp.arange(NR, dtype=jnp.int32)
    growth = 1 + range_index * KMAX // NR
    jitter = jax.random.randint(jax.random.fold_in(key, 23), (NR,), 0, 2)
    jitter = jnp.where(range_index > 0, jitter, 0)
    return jnp.minimum(KMAX, growth + jitter).astype(jnp.int32)


def shard_levels(key, shape, cuts, least, largest):
    loudness, own = 1.0, jax.random.fold_in(key, 6)
    for dim, parts in cuts:
        steps = jnp.exp(jax.random.uniform(jax.random.fold_in(own, dim), (parts,), jnp.float32, least / len(cuts), largest / len(cuts)))
        loudness = loudness * jnp.repeat(steps, shape[dim] // parts).reshape([-1 if axis == dim else 1 for axis in range(len(shape))])
    return loudness


def centred(rng, shape, scale, reach, pieces=(), held_as=jnp.bfloat16):
    drawn = scale * jax.random.normal(rng, shape, jnp.float32)
    if pieces:
        drawn = drawn * shard_levels(rng, shape, pieces, -0.22, 0.18)
    return jnp.clip(drawn, -reach, reach).astype(held_as)


def setup_inputs(seed: int = 0) -> dict:
    key_list = jax.random.split(jax.random.key(seed), 7)
    return {
        "raw": centred(key_list[0], (2, POL, NA, NR), 1.0, 6.0, ((2, 4), (3, 8))),
        "range_chirp": centred(key_list[1], (2, LR), (2 * LR) ** -0.5, 0.25),
        "mig_weight": centred(key_list[2], (2, BW, NR), 0.25, 1.5, ((2, 8),)),
        "mig_offset": draw_mig_offset(jax.random.fold_in(key_list[6], 71), 0),
        "aperture": draw_aperture(jax.random.fold_in(key_list[6], 71), 0),
        "az_rate": jnp.clip(jnp.exp(math.log(1.0) - 1.3862944 * jax.random.uniform(key_list[5], (NR,), jnp.float32) ** shard_levels(key_list[5], (NR,), ((0, 8),), -0.2, 0.2)), 0.25, 1.0),
    }


def kernel_parts(pulse_lag, aper_blocks, az_rates):
    half_len = 64 * aper_blocks
    inside = (pulse_lag >= -half_len) & (pulse_lag < half_len)
    length = (128 * aper_blocks).astype(az_rates.dtype)
    lag_float = pulse_lag.astype(az_rates.dtype)
    phase = math.pi * az_rates * (lag_float * lag_float) / length
    factor = lax.rsqrt(length)
    real_part = jnp.where(inside, jnp.cos(phase) * factor, 0.0)
    imag_part = jnp.where(inside, -jnp.sin(phase) * factor, 0.0)
    return (real_part, imag_part)

def reference(raw, range_chirp, mig_weight, mig_offset, aperture, az_rate):
    range_len = NR + LR
    chirp_float = range_chirp.astype(jnp.float32)
    chirp_spec = jnp.conj(jnp.fft.fft(lax.complex(chirp_float[0], chirp_float[1]), n=range_len))
    weight = mig_weight.astype(jnp.float32)
    band_reach = OFFMAX + BW
    range_index = jnp.arange(NR, dtype=jnp.int32)

    def range_block(block_data):
        values = block_data.astype(jnp.float32)
        spectrum = jnp.fft.fft(lax.complex(values[0], values[1]), n=range_len, axis=-1)
        correlated = jnp.fft.ifft(spectrum * chirp_spec, axis=-1)[..., :NR]
        compressed = jnp.stack([jnp.real(correlated), jnp.imag(correlated)]).astype(jnp.bfloat16)
        padded = jnp.pad(compressed, ((0, 0), (0, 0), (0, 0), (0, band_reach))).astype(jnp.float32)
        real_sum = jnp.zeros(compressed.shape[1:], jnp.float32)
        imag_sum = jnp.zeros(compressed.shape[1:], jnp.float32)
        for band_tap in range(BW):
            picked = jnp.take(padded, (range_index + mig_offset + band_tap).astype(jnp.int32), axis=3)
            weight_real = weight[0, band_tap]
            weight_imag = weight[1, band_tap]
            real_sum = real_sum + weight_real * picked[0] - weight_imag * picked[1]
            imag_sum = imag_sum + weight_real * picked[1] + weight_imag * picked[0]
        return jnp.stack([real_sum, imag_sum]).astype(jnp.bfloat16)
    pulse_blocks = raw.reshape(2, POL, NA // 128, 128, NR).transpose(2, 0, 1, 3, 4)
    migrated = lax.map(range_block, pulse_blocks)
    migrated = migrated.transpose(1, 2, 4, 0, 3).reshape(2, POL, NR, NA)
    azimuth_len = NA + 128 * KMAX
    position = jnp.arange(azimuth_len, dtype=jnp.int32)
    signed_pos = jnp.where(position < azimuth_len // 2, position, position - azimuth_len)
    pulse_lag = -signed_pos
    bin_group = math.gcd(NR, 128)
    range_groups = migrated.reshape(2, POL, NR // bin_group, bin_group, NA).transpose(2, 0, 1, 3, 4)
    aper_groups = aperture.reshape(NR // bin_group, bin_group)
    rate_groups = az_rate.reshape(NR // bin_group, bin_group)

    def azimuth_block(inputs):
        block_data, aper_blocks, az_rates = inputs
        kern_real, kern_imag = kernel_parts(pulse_lag[None, :], aper_blocks[:, None], az_rates[:, None])
        rounded = lax.optimization_barrier((kern_real.astype(jnp.bfloat16), kern_imag.astype(jnp.bfloat16)))
        kern_spec = jnp.fft.fft(lax.complex(rounded[0].astype(jnp.float32), rounded[1].astype(jnp.float32)), axis=-1)
        values = block_data.astype(jnp.float32)
        spectrum = jnp.fft.fft(lax.complex(values[0], values[1]), n=azimuth_len, axis=-1)
        focused = jnp.fft.ifft(spectrum * kern_spec[None], axis=-1)[..., :NA]
        return jnp.stack([jnp.real(focused), jnp.imag(focused)]).astype(jnp.bfloat16)
    image = lax.map(azimuth_block, (range_groups, aper_groups, rate_groups))
    return image.transpose(1, 2, 0, 3, 4).reshape(2, POL, NR, NA)
```

```python
import functools
import math

import jax
import jax.numpy as jnp
from jax import lax
from jax.experimental import pallas as pl
from jax.experimental.pallas import tpu as pltpu
from jax.sharding import PartitionSpec as P

BW = 8
OFFMAX = 120


def passed_along(value, axis, by):
    peers = lax.axis_size(axis)
    pairs = [(i, i + by) for i in range(peers) if 0 <= i + by < peers]
    return lax.ppermute(value, axis, pairs)


def toeplitz_part(taps, row_count, out_cols):
    tap_count = taps.shape[0]
    padded = jnp.concatenate([taps, jnp.zeros((row_count + 1 - tap_count,), taps.dtype)])
    flat = jnp.tile(padded, out_cols)[: out_cols * row_count]
    return flat.reshape(out_cols, row_count).T


def range_matrix(chirp_taps, out_cols):
    tap_count = chirp_taps.shape[1]
    row_count = out_cols + tap_count
    real_part = toeplitz_part(chirp_taps[0], row_count, out_cols)
    imag_part = toeplitz_part(chirp_taps[1], row_count, out_cols)
    upper_half = jnp.concatenate([real_part, -imag_part], axis=1)
    lower_half = jnp.concatenate([imag_part, real_part], axis=1)
    return jnp.concatenate([upper_half, lower_half], axis=0)


def compress(extended, out_cols, chirp_taps):
    stacked = jnp.concatenate([extended[0], extended[1]], axis=-1)
    product = jnp.dot(
        stacked, range_matrix(chirp_taps, out_cols), preferred_element_type=jnp.float32
    )
    return jnp.stack([product[..., :out_cols], product[..., out_cols:]]).astype(jnp.bfloat16)


def migrate(extended, weight, offset, out_cols, band_reach):
    band_taps = weight.shape[1]
    row_count = out_cols + band_reach
    lag_index = (
        jnp.arange(row_count, dtype=jnp.int32)[:, None]
        - jnp.arange(out_cols, dtype=jnp.int32)[None, :]
        - offset[None, :]
    )
    nothing = jnp.zeros((), weight.dtype)
    weight_real = jnp.zeros((row_count, out_cols), weight.dtype)
    weight_imag = jnp.zeros((row_count, out_cols), weight.dtype)
    for band_tap in range(band_taps):
        hit = lag_index == band_tap
        weight_real = weight_real + jnp.where(hit, weight[0, band_tap][None, :], nothing)
        weight_imag = weight_imag + jnp.where(hit, weight[1, band_tap][None, :], nothing)
    upper_half = jnp.concatenate([weight_real, weight_imag], axis=1)
    lower_half = jnp.concatenate([-weight_imag, weight_real], axis=1)
    matrix = jnp.concatenate([upper_half, lower_half], axis=0)
    stacked = jnp.concatenate([extended[0], extended[1]], axis=-1)
    product = jnp.einsum("nps,so->nop", stacked, matrix, preferred_element_type=jnp.float32)
    return jnp.stack([product[:, :out_cols], product[:, out_cols:]]).astype(jnp.bfloat16)


HALF = 4

def az_body(G, S, JL, mode, unroll, x_ref, t_ref, o_ref, F, Z):
    J = S * JL
    R = 4 * J
    NB = 2 * HALF + 1
    F[...] = jnp.zeros_like(F)
    srow = lax.broadcasted_iota(jnp.int32, (128, 128), 0)
    tcol = lax.broadcasted_iota(jnp.int32, (128, 128), 1)
    lower = srow >= tcol

    def one(g, _):
        xf = x_ref[:, g].astype(jnp.float32)
        for s in range(S):
            for cp in range(4):
                F[cp, HALF + JL * s: HALF + JL * (s + 1), :] = xf[s, JL * cp: JL * (cp + 1)]
        lhs = [F[:, d:d + J, :].reshape(R, 128).astype(jnp.bfloat16) for d in range(NB)]
        tiles = []
        for c in range(2):
            segs = t_ref[g, c]
            row = []
            for d in range(2 * HALF):
                if mode == "f32":
                    b = jnp.broadcast_to(segs[d:d + 1], (128, 128))
                    cc = pltpu.roll(b, 0, 1, stride=1, stride_axis=0)
                    row.append(cc)
                else:
                    b = jnp.broadcast_to(segs[d:d + 1], (16, 128))
                    c0 = pltpu.roll(b, 0, 1, stride=1, stride_axis=0).astype(jnp.bfloat16)
                    cc = jnp.concatenate([c0] + [pltpu.roll(c0, 16 * q, 1) for q in range(1, 8)], axis=0)
                    row.append(cc)
            zero = jnp.zeros_like(row[0])
            row = [zero] + row + [zero]
            tiles.append([jnp.where(lower, row[d + 1], row[d]).astype(jnp.bfloat16) for d in range(NB)])
        lhs = jnp.concatenate(lhs, axis=1)
        rhs = jnp.concatenate([jnp.concatenate([tiles[0][d], tiles[1][d]], axis=1) for d in range(NB)], axis=0)
        y = jnp.dot(lhs, rhs, preferred_element_type=jnp.float32)
        H = R // 2
        yre = y[:H, :128] - y[H:, 128:]
        yim = y[:H, 128:] + y[H:, :128]
        for v in range(H // 8):
            Z[pl.ds(g + 8 * v * G, 8, stride=G), :] = yre[8 * v:8 * v + 8]
            Z[pl.ds(g + (H + 8 * v) * G, 8, stride=G), :] = yim[8 * v:8 * v + 8]
        return 0
    lax.fori_loop(0, G, one, 0, unroll=unroll)
    for c in range(2):
        for p in range(2):
            for j in range(J):
                r = (c * 2 + p) * J + j
                o_ref[j // JL, c, p, :, 128 * (j % JL):128 * (j % JL + 1)] = Z[r * G:(r + 1) * G, :].astype(jnp.bfloat16)

def azimuth(x, taps, G=16, mode="f32", unroll=2):
    S, n, rows, _ = x.shape
    JL = rows // 4
    J = S * JL
    return pl.pallas_call(
        functools.partial(az_body, G, S, JL, mode, unroll),
        grid=(n // G,),
        in_specs=[pl.BlockSpec((S, G, rows, 128), lambda i: (0, i, 0, 0)),
                  pl.BlockSpec((G, 2, 2 * HALF, 128), lambda i: (i, 0, 0, 0))],
        out_specs=pl.BlockSpec((S, 2, 2, G, 128 * JL), lambda i: (0, 0, 0, i, 0)),
        out_shape=jax.ShapeDtypeStruct((S, 2, 2, n, 128 * JL), jnp.bfloat16),
        scratch_shapes=[pltpu.VMEM((4, J + 2 * HALF, 128), jnp.float32),
                        pltpu.VMEM((4 * J * G, 128), jnp.float32)],
        compiler_params=pltpu.CompilerParams(vmem_limit_bytes=48 * 2**20),
        name="azimuth",
    )(x, taps)

def taps_of(aper, rate):
    n = aper.shape[0]
    shape = (n, 2 * HALF, 128)
    seg = lax.broadcasted_iota(jnp.int32, shape, 1)
    lane = lax.broadcasted_iota(jnp.int32, shape, 2)
    m = 128 * (seg - HALF) + ((128 - lane) & 127)
    aper = aper[:, None, None]; rate = rate[:, None, None]
    half_len = 64 * aper
    inside = (m >= -half_len) & (m < half_len)
    length = (128 * aper).astype(jnp.float32)
    mf = m.astype(jnp.float32)
    phase = math.pi * rate * (mf * mf) / length
    f = lax.rsqrt(length)
    re = jnp.where(inside, jnp.cos(phase) * f, 0.0)
    im = jnp.where(inside, -jnp.sin(phase) * f, 0.0)
    return jnp.stack([re, im], axis=1)


def shards(raw, range_chirp, mig_weight, mig_offset, aperture, az_rate):
    range_bins = raw.shape[3]
    pulses = raw.shape[2]
    chirp_count = range_chirp.shape[1]
    band_reach = OFFMAX + BW
    raw_tail = passed_along(raw[:, :, :, :chirp_count], "rng", -1)
    compressed = compress(jnp.concatenate([raw, raw_tail], axis=3), range_bins, range_chirp)
    comp_rim = passed_along(compressed[:, :, :, :band_reach], "rng", -1)
    extended = jnp.concatenate([compressed, comp_rim], axis=3)
    migrated = migrate(extended, mig_weight, mig_offset, range_bins, band_reach)
    peers = lax.axis_size("pul")
    local_bins = range_bins // peers
    first_bin = lax.axis_index("pul") * local_bins
    local_blocks = lax.dynamic_slice_in_dim(aperture, first_bin, local_bins)
    local_rates = lax.dynamic_slice_in_dim(az_rate, first_bin, local_bins)
    taps = taps_of(local_blocks, local_rates)
    blocks = pulses // 128
    laid = migrated.reshape(2, 2, peers, local_bins, blocks, 128).transpose(2, 3, 0, 1, 4, 5)
    laid = laid.reshape(peers, local_bins, 4 * blocks, 128)
    laid = lax.all_to_all(laid, "pul", split_axis=0, concat_axis=0, tiled=True)
    focused = azimuth(laid, taps, G=min(16, local_bins), mode="f32", unroll=2)
    focused = lax.all_to_all(focused, "pul", split_axis=0, concat_axis=0, tiled=True)
    return focused.transpose(1, 2, 0, 3, 4).reshape(2, 2, range_bins, pulses)


def solution(mesh):
    placed = (P(None, None, "pul", "rng"), P(), P(None, None, "rng"), P("rng"), P("rng"), P("rng"))
    return jax.shard_map(
        shards, mesh=mesh, in_specs=placed, out_specs=P(None, None, "rng", "pul"), check_vma=False
    )
```

```python
import functools
import math

import jax
import jax.numpy as jnp
from jax import lax
from jax.experimental import pallas as pl
from jax.experimental.pallas import tpu as pltpu
from jax.sharding import PartitionSpec as P

OFFMAX = 120
SPLIT = (2, 2)


def passed_along(value, axis, by):
    peers = lax.axis_size(axis)
    pairs = [(i, i + by) for i in range(peers) if 0 <= i + by < peers]
    return lax.ppermute(value, axis, pairs)


BW = 8

def s1_body(first, count, peers, starts, me_ref, chirp_ref, w_ref, off_ref, *refs):
    srcs, o_refs, Z = refs[:len(starts)], refs[len(starts):-1], refs[-1]
    pulses = srcs[0].shape[2]
    tap_count = chirp_ref.shape[1]
    JL = pulses // 128
    span = tap_count // 128 + 1
    wide = 128 * span
    parts = []
    for c in range(2):
        row = chirp_ref[c:c + 1, :].astype(jnp.float32)
        row = jnp.concatenate([row, jnp.zeros((1, 128), jnp.float32)], axis=1)
        parts.append(pltpu.roll(jnp.broadcast_to(row, (128, wide)), 0, 1, stride=1, stride_axis=0))
    re, im = (v.astype(jnp.bfloat16) for v in parts)
    corr = jnp.concatenate([jnp.concatenate([re, im], axis=1), jnp.concatenate([-im, re], axis=1)], axis=0)

    def block(c, p, b):
        for ref, start in zip(srcs, starts):
            if start <= b < start + ref.shape[3] // 128:
                return ref[c, p, :, 128 * (b - start):128 * (b - start) + 128]

    def compressed(b):
        cols = []
        for p in range(2):
            win = jnp.concatenate([block(c, p, b + i) for c in range(2) for i in range(span)], axis=1)
            cols.append(lax.dot_general(corr, win, (((1,), (1,)), ((), ())), preferred_element_type=jnp.float32).astype(jnp.bfloat16))
        return jnp.concatenate(cols, axis=1)

    now = compressed(first)
    for q in range(count):
        nxt = compressed(first + q + 1)
        cols = [w_ref[0, :, 128 * q:128 * q + 128].astype(jnp.float32),
                w_ref[1, :, 128 * q:128 * q + 128].astype(jnp.float32),
                jnp.broadcast_to(off_ref[:, 128 * q:128 * q + 128].astype(jnp.float32), (8, 128)),
                jnp.zeros((128 - 3 * BW, 128), jnp.float32)]
        tab = jnp.concatenate(cols, axis=0).T
        lag = (lax.broadcasted_iota(jnp.int32, (128, 256), 1) - lax.broadcasted_iota(jnp.int32, (128, 256), 0)).astype(jnp.float32) - tab[:, 2 * BW:2 * BW + 1]
        wr = jnp.zeros((128, 256), jnp.float32)
        wi = jnp.zeros((128, 256), jnp.float32)
        for b in range(BW):
            hit = lag == float(b)
            wr = jnp.where(hit, tab[:, b:b + 1], wr)
            wi = jnp.where(hit, tab[:, BW + b:BW + b + 1], wi)
        wr = wr.astype(jnp.bfloat16)
        wi = wi.astype(jnp.bfloat16)
        top = jnp.concatenate([wr[:, :128], -wi[:, :128], wr[:, 128:], -wi[:, 128:]], axis=1)
        low = jnp.concatenate([wi[:, :128], wr[:, :128], wi[:, 128:], wr[:, 128:]], axis=1)
        lhs = jnp.concatenate([top, low], axis=0)
        rhs = jnp.concatenate([now, nxt], axis=0)
        y = jnp.dot(lhs, rhs, preferred_element_type=jnp.float32)
        R = 4 * JL
        for c in range(2):
            for p in range(2):
                for j in range(JL):
                    k = (2 * c + p) * JL + j
                    for t in range(16):
                        Z[pl.ds((128 * q + 8 * t) * R + k, 8, stride=R), :] = y[128 * c + 8 * t:128 * c + 8 * t + 8, (p * JL + j) * 128:(p * JL + j + 1) * 128]
        now = nxt
    own = 128 * count // peers
    for k in range(peers):
        start = pl.multiple_of((me_ref[0] ^ k) * (own * R), own * R)
        o_refs[k][...] = Z[pl.ds(start, own * R), :].reshape(own, R, 128).astype(jnp.bfloat16)

def stage1(me, sources, chirp, weight, offset, first, count, peers):
    pulses = sources[0][0].shape[2]
    rows = 4 * pulses // 128
    own = 128 * count // peers
    last = first + count + chirp.shape[1] // 128
    specs, starts, values = [], [], []
    for value, start in sources:
        blocks = value.shape[3] // 128
        if start > last or start + blocks <= first:
            continue
        skip = max(0, first - start)
        width = blocks - skip
        if skip % width:
            skip, width = 0, blocks
        specs.append(pl.BlockSpec((2, 2, pulses, 128 * width), functools.partial(lambda n, i: (0, 0, 0, n), skip // width)))
        starts.append(start + skip)
        values.append(value)
    whole = lambda shape: pl.BlockSpec(shape, lambda i: (0,) * len(shape))
    w = weight[:, :, 128 * first:128 * (first + count)]
    off = offset.reshape(1, -1)[:, 128 * first:128 * (first + count)]
    return pl.pallas_call(
        functools.partial(s1_body, first, count, peers, tuple(starts)),
        grid=(1,),
        out_shape=[jax.ShapeDtypeStruct((own, rows, 128), jnp.bfloat16)] * peers,
        in_specs=[pl.BlockSpec(memory_space=pltpu.SMEM), whole(chirp.shape), whole(w.shape), whole(off.shape)] + specs,
        out_specs=[whole((own, rows, 128))] * peers,
        scratch_shapes=[pltpu.VMEM((128 * count * rows, 128), jnp.float32)],
        compiler_params=pltpu.CompilerParams(vmem_limit_bytes=48 * 2**20),
        name="range_stage",
    )(me, chirp, w, off, *values)


HALF = 4

def taps_of(aper, rate):
    n = aper.shape[0]
    shape = (n, 2 * HALF, 128)
    seg = lax.broadcasted_iota(jnp.int32, shape, 1)
    lane = lax.broadcasted_iota(jnp.int32, shape, 2)
    m = 128 * (seg - HALF) + ((128 - lane) & 127)
    aper = aper[:, None, None]; rate = rate[:, None, None]
    half_len = 64 * aper
    inside = (m >= -half_len) & (m < half_len)
    length = (128 * aper).astype(jnp.float32)
    mf = m.astype(jnp.float32)
    phase = math.pi * rate * (mf * mf) / length
    f = lax.rsqrt(length)
    re = jnp.where(inside, jnp.cos(phase) * f, 0.0)
    im = jnp.where(inside, -jnp.sin(phase) * f, 0.0)
    return jnp.stack([re, im], axis=1)


def az_body(G, S, JL, me_ref, t_ref, *refs):
    x_refs, o_refs, (F, Z) = refs[:S], refs[S:2 * S], refs[2 * S:]
    me = me_ref[0]
    J = S * JL
    R = 4 * J
    H = R // 2
    NB = 2 * HALF + 1
    for k in range(S):
        src = me ^ k
        part = x_refs[k][...].astype(jnp.float32)
        for cp in range(4):
            F[:, cp, pl.ds(HALF + JL * src, JL), :] = part[:, JL * cp:JL * cp + JL]
    edge = jnp.zeros((G, 4, HALF, 128), jnp.float32)
    F[:, :, 0:HALF, :] = edge
    F[:, :, HALF + J:, :] = edge
    lower = lax.broadcasted_iota(jnp.int32, (128, 128), 0) >= lax.broadcasted_iota(jnp.int32, (128, 128), 1)

    def toeplitz(g, c):
        segs = t_ref[g, c]
        row = []
        for d in range(2 * HALF):
            b = jnp.broadcast_to(segs[d:d + 1], (128, 128))
            row.append(pltpu.roll(b, 0, 1, stride=1, stride_axis=0).astype(jnp.bfloat16))
        zero = jnp.zeros_like(row[0])
        row = [zero] + row + [zero]
        return [jnp.where(lower, row[d + 1], row[d]) for d in range(NB)]

    def one(g, _):
        lhs = [F[g, :, d:d + J, :].reshape(R, 128).astype(jnp.bfloat16) for d in range(NB)]
        re, im = toeplitz(g, 0), toeplitz(g, 1)
        rhs = jnp.concatenate([jnp.concatenate([re[d], im[d]], axis=1) for d in range(NB)], axis=0)
        y = jnp.dot(jnp.concatenate(lhs, axis=1), rhs, preferred_element_type=jnp.float32)
        yre = y[:H, :128] - y[H:, 128:]
        yim = y[:H, 128:] + y[H:, :128]
        for v in range(H // 8):
            Z[pl.ds(g + 8 * v * G, 8, stride=G), :] = yre[8 * v:8 * v + 8]
            Z[pl.ds(g + (H + 8 * v) * G, 8, stride=G), :] = yim[8 * v:8 * v + 8]
        return 0

    lax.fori_loop(0, G, one, 0, unroll=4)
    for k in range(S):
        src = me ^ k
        for cp in range(4):
            for j in range(JL):
                r = pl.multiple_of((cp * J + JL * src + j) * G, G)
                o_refs[k][cp // 2, cp % 2, :, 128 * j:128 * j + 128] = Z[pl.ds(r, G), :].astype(jnp.bfloat16)


def azimuth(me, taps, *xs):
    S = len(xs)
    n, rows, _ = xs[0].shape
    JL = rows // 4
    J = S * JL
    G = min(16, n)
    return pl.pallas_call(
        functools.partial(az_body, G, S, JL),
        grid=(n // G,),
        in_specs=[pl.BlockSpec(memory_space=pltpu.SMEM), pl.BlockSpec((G, 2, 2 * HALF, 128), lambda i: (i, 0, 0, 0))]
        + [pl.BlockSpec((G, rows, 128), lambda i: (i, 0, 0))] * S,
        out_specs=[pl.BlockSpec((2, 2, G, 128 * JL), lambda i: (0, 0, i, 0))] * S,
        out_shape=[jax.ShapeDtypeStruct((2, 2, n, 128 * JL), jnp.bfloat16)] * S,
        scratch_shapes=[pltpu.VMEM((G, 4, J + 2 * HALF, 128), jnp.float32),
                        pltpu.VMEM((4 * J * G, 128), jnp.float32)],
        compiler_params=pltpu.CompilerParams(vmem_limit_bytes=48 * 2**20),
        name="azimuth",
    )(me, taps, *xs)


def assemble(me, pieces, peers, bins, pulses):
    def body(*refs):
        me_ref, spots, image, sem = refs[0], refs[1:-2], refs[-2], refs[-1]
        copies = []
        base = 0
        for n, piece in enumerate(spots):
            width = piece.shape[2]
            start = pl.multiple_of(base + (me_ref[0] ^ (n % peers)) * width, 16)
            copies.append(pltpu.make_async_copy(piece, image.at[:, :, pl.ds(start, width), :], sem.at[n]))
            if n % peers == peers - 1:
                base += width * peers
        for copy in copies:
            copy.start()
        for copy in copies:
            copy.wait()

    return pl.pallas_call(
        body,
        out_shape=jax.ShapeDtypeStruct((2, 2, bins, pulses), jnp.bfloat16),
        in_specs=[pl.BlockSpec(memory_space=pltpu.SMEM)] + [pl.BlockSpec(memory_space=pl.ANY)] * len(pieces),
        out_specs=pl.BlockSpec(memory_space=pl.ANY),
        scratch_shapes=[pltpu.SemaphoreType.DMA((len(pieces),))],
        name="assemble",
    )(me, *pieces)


def swap(pieces):
    peers = len(pieces)
    out = [pieces[0]]
    for k in range(1, peers):
        out.append(lax.ppermute(pieces[k], "pul", [(i, i ^ k) for i in range(peers)]))
    return out


def shards(raw, range_chirp, mig_weight, mig_offset, aperture, az_rate):
    bins = raw.shape[3]
    pulses = raw.shape[2]
    peers = lax.axis_size("pul")
    me = lax.axis_index("pul").astype(jnp.int32).reshape(1)
    blocks = bins // 128
    reach = range_chirp.shape[1] // 128 + (OFFMAX + BW) // 128
    sources = [(raw, 0)]
    got = 0
    first = 0
    sent = []
    for count in SPLIT:
        need = min(reach, first + count + reach - blocks)
        if need > got:
            piece = passed_along(raw[:, :, :, 128 * got:128 * need], "rng", -1)
            sources.append((piece, blocks + got))
            got = need
        first_piece = stage1(me, sources, range_chirp, mig_weight, mig_offset, first, count, peers)
        sent.append((first, count, first_piece))
        first += count
    arrived = [(first, count, swap(pieces)) for first, count, pieces in sent]
    back = []
    for first, count, pieces in arrived:
        own = 128 * count // peers
        begin = 128 * first + me[0] * own
        taps = taps_of(lax.dynamic_slice_in_dim(aperture, begin, own), lax.dynamic_slice_in_dim(az_rate, begin, own))
        back += swap(azimuth(me, taps, *pieces))
    return assemble(me, back, peers, bins, pulses)


def solution(mesh):
    placed = (P(None, None, "pul", "rng"), P(), P(None, None, "rng"), P("rng"), P("rng"), P("rng"))
    return jax.shard_map(
        shards, mesh=mesh, in_specs=placed, out_specs=P(None, None, "rng", "pul"), check_vma=False
    )
```

```python
import functools
import math

import jax
import jax.numpy as jnp
from jax import lax
from jax.experimental import pallas as pl
from jax.experimental.pallas import tpu as pltpu
from jax.sharding import PartitionSpec as P

OFFMAX = 120
SPLIT = (2, 2)
LAST = 4


def passed_along(value, axis, by):
    peers = lax.axis_size(axis)
    pairs = [(i, i + by) for i in range(peers) if 0 <= i + by < peers]
    return lax.ppermute(value, axis, pairs)


BW = 8

def s1_body(first, count, peers, starts, me_ref, chirp_ref, w_ref, off_ref, *refs):
    srcs, o_refs, Z = refs[:len(starts)], refs[len(starts):-1], refs[-1]
    pulses = srcs[0].shape[2]
    tap_count = chirp_ref.shape[1]
    JL = pulses // 128
    span = tap_count // 128 + 1
    wide = 128 * span
    parts = []
    for c in range(2):
        row = chirp_ref[c:c + 1, :].astype(jnp.float32)
        row = jnp.concatenate([row, jnp.zeros((1, 128), jnp.float32)], axis=1)
        parts.append(pltpu.roll(jnp.broadcast_to(row, (128, wide)), 0, 1, stride=1, stride_axis=0))
    re, im = (v.astype(jnp.bfloat16) for v in parts)
    corr = jnp.concatenate([jnp.concatenate([re, im], axis=1), jnp.concatenate([-im, re], axis=1)], axis=0)

    def block(c, p, b):
        for ref, start in zip(srcs, starts):
            if start <= b < start + ref.shape[3] // 128:
                return ref[c, p, :, 128 * (b - start):128 * (b - start) + 128]

    def compressed(b):
        cols = []
        for p in range(2):
            win = jnp.concatenate([block(c, p, b + i) for c in range(2) for i in range(span)], axis=1)
            cols.append(lax.dot_general(corr, win, (((1,), (1,)), ((), ())), preferred_element_type=jnp.float32).astype(jnp.bfloat16))
        return jnp.concatenate(cols, axis=1)

    now = compressed(first)
    for q in range(count):
        nxt = compressed(first + q + 1)
        cols = [w_ref[0, :, 128 * q:128 * q + 128].astype(jnp.float32),
                w_ref[1, :, 128 * q:128 * q + 128].astype(jnp.float32),
                jnp.broadcast_to(off_ref[:, 128 * q:128 * q + 128].astype(jnp.float32), (8, 128)),
                jnp.zeros((128 - 3 * BW, 128), jnp.float32)]
        tab = jnp.concatenate(cols, axis=0).T
        lag = (lax.broadcasted_iota(jnp.int32, (128, 256), 1) - lax.broadcasted_iota(jnp.int32, (128, 256), 0)).astype(jnp.float32) - tab[:, 2 * BW:2 * BW + 1]
        wr = jnp.zeros((128, 256), jnp.float32)
        wi = jnp.zeros((128, 256), jnp.float32)
        for b in range(BW):
            hit = lag == float(b)
            wr = jnp.where(hit, tab[:, b:b + 1], wr)
            wi = jnp.where(hit, tab[:, BW + b:BW + b + 1], wi)
        wr = wr.astype(jnp.bfloat16)
        wi = wi.astype(jnp.bfloat16)
        top = jnp.concatenate([wr[:, :128], -wi[:, :128], wr[:, 128:], -wi[:, 128:]], axis=1)
        low = jnp.concatenate([wi[:, :128], wr[:, :128], wi[:, 128:], wr[:, 128:]], axis=1)
        lhs = jnp.concatenate([top, low], axis=0)
        rhs = jnp.concatenate([now, nxt], axis=0)
        y = jnp.dot(lhs, rhs, preferred_element_type=jnp.float32)
        R = 4 * JL
        for c in range(2):
            for p in range(2):
                for j in range(JL):
                    k = (2 * c + p) * JL + j
                    for t in range(16):
                        Z[pl.ds((128 * q + 8 * t) * R + k, 8, stride=R), :] = y[128 * c + 8 * t:128 * c + 8 * t + 8, (p * JL + j) * 128:(p * JL + j + 1) * 128]
        now = nxt
    own = 128 * count // peers
    for k in range(peers):
        start = pl.multiple_of((me_ref[0] ^ k) * (own * R), own * R)
        o_refs[k][...] = Z[pl.ds(start, own * R), :].reshape(own, R, 128).astype(jnp.bfloat16)

def stage1(me, sources, chirp, weight, offset, first, count, peers):
    pulses = sources[0][0].shape[2]
    rows = 4 * pulses // 128
    own = 128 * count // peers
    last = first + count + chirp.shape[1] // 128
    specs, starts, values = [], [], []
    for value, start in sources:
        blocks = value.shape[3] // 128
        if start > last or start + blocks <= first:
            continue
        skip = max(0, first - start)
        width = blocks - skip
        if skip % width:
            skip, width = 0, blocks
        specs.append(pl.BlockSpec((2, 2, pulses, 128 * width), functools.partial(lambda n, i: (0, 0, 0, n), skip // width)))
        starts.append(start + skip)
        values.append(value)
    whole = lambda shape: pl.BlockSpec(shape, lambda i: (0,) * len(shape))
    w = weight[:, :, 128 * first:128 * (first + count)]
    off = offset.reshape(1, -1)[:, 128 * first:128 * (first + count)]
    return pl.pallas_call(
        functools.partial(s1_body, first, count, peers, tuple(starts)),
        grid=(1,),
        out_shape=[jax.ShapeDtypeStruct((own, rows, 128), jnp.bfloat16)] * peers,
        in_specs=[pl.BlockSpec(memory_space=pltpu.SMEM), whole(chirp.shape), whole(w.shape), whole(off.shape)] + specs,
        out_specs=[whole((own, rows, 128))] * peers,
        scratch_shapes=[pltpu.VMEM((128 * count * rows, 128), jnp.float32)],
        compiler_params=pltpu.CompilerParams(vmem_limit_bytes=48 * 2**20),
        name="range_stage",
    )(me, chirp, w, off, *values)


HALF = 4

def taps_of(aper, rate):
    n = aper.shape[0]
    shape = (n, 2 * HALF, 128)
    seg = lax.broadcasted_iota(jnp.int32, shape, 1)
    lane = lax.broadcasted_iota(jnp.int32, shape, 2)
    m = 128 * (seg - HALF) + ((128 - lane) & 127)
    aper = aper[:, None, None]; rate = rate[:, None, None]
    half_len = 64 * aper
    inside = (m >= -half_len) & (m < half_len)
    length = (128 * aper).astype(jnp.float32)
    mf = m.astype(jnp.float32)
    phase = math.pi * rate * (mf * mf) / length
    f = lax.rsqrt(length)
    re = jnp.where(inside, jnp.cos(phase) * f, 0.0)
    im = jnp.where(inside, -jnp.sin(phase) * f, 0.0)
    return jnp.stack([re, im], axis=1)


def az_body(G, S, JL, me_ref, t_ref, *refs):
    x_refs, o_refs, (F, Z) = refs[:S], refs[S:2 * S], refs[2 * S:]
    me = me_ref[0]
    J = S * JL
    R = 4 * J
    H = R // 2
    NB = 2 * HALF + 1
    for k in range(S):
        src = me ^ k
        part = x_refs[k][...].astype(jnp.float32)
        for cp in range(4):
            F[:, cp, pl.ds(HALF + JL * src, JL), :] = part[:, JL * cp:JL * cp + JL]
    edge = jnp.zeros((G, 4, HALF, 128), jnp.float32)
    F[:, :, 0:HALF, :] = edge
    F[:, :, HALF + J:, :] = edge
    lower = lax.broadcasted_iota(jnp.int32, (128, 128), 0) >= lax.broadcasted_iota(jnp.int32, (128, 128), 1)

    def toeplitz(g, c):
        segs = t_ref[g, c]
        row = []
        for d in range(2 * HALF):
            b = jnp.broadcast_to(segs[d:d + 1], (128, 128))
            row.append(pltpu.roll(b, 0, 1, stride=1, stride_axis=0).astype(jnp.bfloat16))
        zero = jnp.zeros_like(row[0])
        row = [zero] + row + [zero]
        return [jnp.where(lower, row[d + 1], row[d]) for d in range(NB)]

    def one(g, _):
        lhs = [F[g, :, d:d + J, :].reshape(R, 128).astype(jnp.bfloat16) for d in range(NB)]
        re, im = toeplitz(g, 0), toeplitz(g, 1)
        rhs = jnp.concatenate([jnp.concatenate([re[d], im[d]], axis=1) for d in range(NB)], axis=0)
        y = jnp.dot(jnp.concatenate(lhs, axis=1), rhs, preferred_element_type=jnp.float32)
        yre = y[:H, :128] - y[H:, 128:]
        yim = y[:H, 128:] + y[H:, :128]
        for v in range(H // 8):
            Z[pl.ds(g + 8 * v * G, 8, stride=G), :] = yre[8 * v:8 * v + 8]
            Z[pl.ds(g + (H + 8 * v) * G, 8, stride=G), :] = yim[8 * v:8 * v + 8]
        return 0

    lax.fori_loop(0, G, one, 0, unroll=max(1, min(G, 64 // S)))
    for k in range(S):
        src = me ^ k
        for cp in range(4):
            for j in range(JL):
                r = pl.multiple_of((cp * J + JL * src + j) * G, G)
                o_refs[k][cp // 2, cp % 2, :, 128 * j:128 * j + 128] = Z[pl.ds(r, G), :].astype(jnp.bfloat16)


def azimuth(me, taps, xs, begin, end):
    S = len(xs)
    rows = xs[0].shape[1]
    JL = rows // 4
    J = S * JL
    G = min(16, end - begin)
    skip = begin // G
    return pl.pallas_call(
        functools.partial(az_body, G, S, JL),
        grid=((end - begin) // G,),
        in_specs=[pl.BlockSpec(memory_space=pltpu.SMEM), pl.BlockSpec((G, 2, 2 * HALF, 128), lambda i: (i + skip, 0, 0, 0))]
        + [pl.BlockSpec((G, rows, 128), lambda i: (i + skip, 0, 0))] * S,
        out_specs=[pl.BlockSpec((2, 2, G, 128 * JL), lambda i: (0, 0, i, 0))] * S,
        out_shape=[jax.ShapeDtypeStruct((2, 2, end - begin, 128 * JL), jnp.bfloat16)] * S,
        scratch_shapes=[pltpu.VMEM((G, 4, J + 2 * HALF, 128), jnp.float32),
                        pltpu.VMEM((4 * J * G, 128), jnp.float32)],
        compiler_params=pltpu.CompilerParams(vmem_limit_bytes=48 * 2**20),
        name="azimuth",
    )(me, taps, *xs)


def assemble(me, pieces, image, first, stride, bins, pulses):
    peers = len(pieces)
    width = pieces[0].shape[2]
    kept = [] if image is None else [image]

    def body(me_ref, *refs):
        spots, out, sem = refs[:peers], refs[-2], refs[-1]
        copies = []
        for k, piece in enumerate(spots):
            start = pl.multiple_of(first + (me_ref[0] ^ k) * stride, 16)
            for n in range(4):
                spot = out.at[n // 2, n % 2, pl.ds(start, width), :]
                copies.append(pltpu.make_async_copy(piece.at[n // 2, n % 2], spot, sem.at[4 * k + n]))
        for copy in copies:
            copy.start()
        for copy in copies:
            copy.wait()

    return pl.pallas_call(
        body,
        out_shape=jax.ShapeDtypeStruct((2, 2, bins, pulses), jnp.bfloat16),
        in_specs=[pl.BlockSpec(memory_space=pltpu.SMEM)] + [pl.BlockSpec(memory_space=pltpu.VMEM)] * peers
        + [pl.BlockSpec(memory_space=pl.ANY)] * len(kept),
        out_specs=pl.BlockSpec(memory_space=pl.ANY),
        scratch_shapes=[pltpu.SemaphoreType.DMA((4 * peers,))],
        input_output_aliases={peers + 1: 0} if kept else {},
        name="assemble",
    )(me, *pieces, *kept)


def swap(pieces):
    peers = len(pieces)
    out = [pieces[0]]
    for k in range(1, peers):
        out.append(lax.ppermute(pieces[k], "pul", [(i, i ^ k) for i in range(peers)]))
    return out


def shards(raw, range_chirp, mig_weight, mig_offset, aperture, az_rate):
    bins = raw.shape[3]
    pulses = raw.shape[2]
    peers = lax.axis_size("pul")
    me = lax.axis_index("pul").astype(jnp.int32).reshape(1)
    blocks = bins // 128
    reach = range_chirp.shape[1] // 128 + (OFFMAX + BW) // 128
    sources = [(raw, 0)]
    got = 0
    first = 0
    sent = []
    for count in SPLIT:
        need = min(reach, first + count + reach - blocks)
        if need > got:
            piece = passed_along(raw[:, :, :, 128 * got:128 * need], "rng", -1)
            sources.append((piece, blocks + got))
            got = need
        first_piece = stage1(me, sources, range_chirp, mig_weight, mig_offset, first, count, peers)
        sent.append((first, count, first_piece))
        first += count
    arrived = [(first, count, swap(pieces)) for first, count, pieces in sent]
    back = []
    for first, count, pieces in arrived:
        own = 128 * count // peers
        begin = 128 * first + me[0] * own
        taps = taps_of(lax.dynamic_slice_in_dim(aperture, begin, own), lax.dynamic_slice_in_dim(az_rate, begin, own))
        cuts = [0, own]
        if first + count == blocks and own > 16 * LAST:
            cuts = [0, own - 16 * LAST, own]
        for cut, end in zip(cuts, cuts[1:]):
            back.append((128 * first + cut, own, swap(azimuth(me, taps, pieces, cut, end))))
    image = None
    for start, own, pieces in back:
        image = assemble(me, pieces, image, start, own, bins, pulses)
    return image


def solution(mesh):
    placed = (P(None, None, "pul", "rng"), P(), P(None, None, "rng"), P("rng"), P("rng"), P("rng"))
    return jax.shard_map(
        shards, mesh=mesh, in_specs=placed, out_specs=P(None, None, "rng", "pul"), check_vma=False
    )
```

```python
import functools
import math

import jax
import jax.numpy as jnp
from jax import lax
from jax.experimental import pallas as pl
from jax.experimental.pallas import tpu as pltpu
from jax.sharding import PartitionSpec as P

OFFMAX = 120
SPLIT = (2, 2)
LAST = 1


def passed_along(value, axis, by):
    peers = lax.axis_size(axis)
    pairs = [(i, i + by) for i in range(peers) if 0 <= i + by < peers]
    return lax.ppermute(value, axis, pairs)


BW = 8

def s1_body(first, count, peers, starts, me_ref, chirp_ref, w_ref, off_ref, *refs):
    srcs, o_refs, Z = refs[:len(starts)], refs[len(starts):-1], refs[-1]
    pulses = srcs[0].shape[2]
    tap_count = chirp_ref.shape[1]
    JL = pulses // 128
    span = tap_count // 128 + 1
    wide = 128 * span
    parts = []
    for c in range(2):
        row = chirp_ref[c:c + 1, :].astype(jnp.float32)
        row = jnp.concatenate([row, jnp.zeros((1, 128), jnp.float32)], axis=1)
        parts.append(pltpu.roll(jnp.broadcast_to(row, (128, wide)), 0, 1, stride=1, stride_axis=0))
    re, im = (v.astype(jnp.bfloat16) for v in parts)
    corr = jnp.concatenate([jnp.concatenate([re, im], axis=1), jnp.concatenate([-im, re], axis=1)], axis=0)

    def block(c, p, b):
        for ref, start in zip(srcs, starts):
            if start <= b < start + ref.shape[3] // 128:
                return ref[c, p, :, 128 * (b - start):128 * (b - start) + 128]

    def compressed(b):
        cols = []
        for p in range(2):
            win = jnp.concatenate([block(c, p, b + i) for c in range(2) for i in range(span)], axis=1)
            cols.append(lax.dot_general(corr, win, (((1,), (1,)), ((), ())), preferred_element_type=jnp.float32).astype(jnp.bfloat16))
        return jnp.concatenate(cols, axis=1)

    now = compressed(first)
    for q in range(count):
        nxt = compressed(first + q + 1)
        cols = [w_ref[0, :, 128 * q:128 * q + 128].astype(jnp.float32),
                w_ref[1, :, 128 * q:128 * q + 128].astype(jnp.float32),
                jnp.broadcast_to(off_ref[:, 128 * q:128 * q + 128].astype(jnp.float32), (8, 128)),
                jnp.zeros((128 - 3 * BW, 128), jnp.float32)]
        tab = jnp.concatenate(cols, axis=0).T
        lag = (lax.broadcasted_iota(jnp.int32, (128, 256), 1) - lax.broadcasted_iota(jnp.int32, (128, 256), 0)).astype(jnp.float32) - tab[:, 2 * BW:2 * BW + 1]
        wr = jnp.zeros((128, 256), jnp.float32)
        wi = jnp.zeros((128, 256), jnp.float32)
        for b in range(BW):
            hit = lag == float(b)
            wr = jnp.where(hit, tab[:, b:b + 1], wr)
            wi = jnp.where(hit, tab[:, BW + b:BW + b + 1], wi)
        wr = wr.astype(jnp.bfloat16)
        wi = wi.astype(jnp.bfloat16)
        top = jnp.concatenate([wr[:, :128], -wi[:, :128], wr[:, 128:], -wi[:, 128:]], axis=1)
        low = jnp.concatenate([wi[:, :128], wr[:, :128], wi[:, 128:], wr[:, 128:]], axis=1)
        lhs = jnp.concatenate([top, low], axis=0)
        rhs = jnp.concatenate([now, nxt], axis=0)
        y = jnp.dot(lhs, rhs, preferred_element_type=jnp.float32)
        R = 4 * JL
        for c in range(2):
            for p in range(2):
                for j in range(JL):
                    k = (2 * c + p) * JL + j
                    for t in range(16):
                        Z[pl.ds((128 * q + 8 * t) * R + k, 8, stride=R), :] = y[128 * c + 8 * t:128 * c + 8 * t + 8, (p * JL + j) * 128:(p * JL + j + 1) * 128]
        now = nxt
    own = 128 * count // peers
    for k in range(peers):
        start = pl.multiple_of((me_ref[0] ^ k) * (own * R), own * R)
        o_refs[k][...] = Z[pl.ds(start, own * R), :].reshape(own, R, 128).astype(jnp.bfloat16)

def stage1(me, sources, chirp, weight, offset, first, count, peers):
    pulses = sources[0][0].shape[2]
    rows = 4 * pulses // 128
    own = 128 * count // peers
    last = first + count + chirp.shape[1] // 128
    specs, starts, values = [], [], []
    for value, start in sources:
        blocks = value.shape[3] // 128
        if start > last or start + blocks <= first:
            continue
        skip = max(0, first - start)
        width = blocks - skip
        if skip % width:
            skip, width = 0, blocks
        specs.append(pl.BlockSpec((2, 2, pulses, 128 * width), functools.partial(lambda n, i: (0, 0, 0, n), skip // width)))
        starts.append(start + skip)
        values.append(value)
    whole = lambda shape: pl.BlockSpec(shape, lambda i: (0,) * len(shape))
    w = weight[:, :, 128 * first:128 * (first + count)]
    off = offset.reshape(1, -1)[:, 128 * first:128 * (first + count)]
    return pl.pallas_call(
        functools.partial(s1_body, first, count, peers, tuple(starts)),
        grid=(1,),
        out_shape=[jax.ShapeDtypeStruct((own, rows, 128), jnp.bfloat16)] * peers,
        in_specs=[pl.BlockSpec(memory_space=pltpu.SMEM), whole(chirp.shape), whole(w.shape), whole(off.shape)] + specs,
        out_specs=[whole((own, rows, 128))] * peers,
        scratch_shapes=[pltpu.VMEM((128 * count * rows, 128), jnp.float32)],
        compiler_params=pltpu.CompilerParams(vmem_limit_bytes=24 * 2**20),
        cost_estimate=pl.CostEstimate(flops=int(1.38e+10 if first == 0 else 4.37e+09), bytes_accessed=4 << 20, transcendentals=0),
        name="range_stage",
    )(me, chirp, w, off, *values)


HALF = 4

def taps_of(aper, rate):
    n = aper.shape[0]
    shape = (n, 2 * HALF, 128)
    seg = lax.broadcasted_iota(jnp.int32, shape, 1)
    lane = lax.broadcasted_iota(jnp.int32, shape, 2)
    m = 128 * (seg - HALF) + ((128 - lane) & 127)
    aper = aper[:, None, None]; rate = rate[:, None, None]
    half_len = 64 * aper
    inside = (m >= -half_len) & (m < half_len)
    length = (128 * aper).astype(jnp.float32)
    mf = m.astype(jnp.float32)
    phase = math.pi * rate * (mf * mf) / length
    f = lax.rsqrt(length)
    re = jnp.where(inside, jnp.cos(phase) * f, 0.0)
    im = jnp.where(inside, -jnp.sin(phase) * f, 0.0)
    return jnp.stack([re, im], axis=1)


def az_body(G, S, JL, me_ref, t_ref, *refs):
    x_refs, o_refs, (F, Z) = refs[:S], refs[S:2 * S], refs[2 * S:]
    me = me_ref[0]
    J = S * JL
    R = 4 * J
    H = R // 2
    NB = 2 * HALF + 1
    for k in range(S):
        src = me ^ k
        part = x_refs[k][...].astype(jnp.float32)
        for cp in range(4):
            F[:, cp, pl.ds(HALF + JL * src, JL), :] = part[:, JL * cp:JL * cp + JL]
    edge = jnp.zeros((G, 4, HALF, 128), jnp.float32)
    F[:, :, 0:HALF, :] = edge
    F[:, :, HALF + J:, :] = edge
    lower = lax.broadcasted_iota(jnp.int32, (128, 128), 0) >= lax.broadcasted_iota(jnp.int32, (128, 128), 1)

    def toeplitz(g, c):
        segs = t_ref[g, c]
        row = []
        for d in range(2 * HALF):
            b = jnp.broadcast_to(segs[d:d + 1], (128, 128))
            row.append(pltpu.roll(b, 0, 1, stride=1, stride_axis=0).astype(jnp.bfloat16))
        zero = jnp.zeros_like(row[0])
        row = [zero] + row + [zero]
        return [jnp.where(lower, row[d + 1], row[d]) for d in range(NB)]

    def one(g, _):
        lhs = [F[g, :, d:d + J, :].reshape(R, 128).astype(jnp.bfloat16) for d in range(NB)]
        re, im = toeplitz(g, 0), toeplitz(g, 1)
        rhs = jnp.concatenate([jnp.concatenate([re[d], im[d]], axis=1) for d in range(NB)], axis=0)
        y = jnp.dot(jnp.concatenate(lhs, axis=1), rhs, preferred_element_type=jnp.float32)
        yre = y[:H, :128] - y[H:, 128:]
        yim = y[:H, 128:] + y[H:, :128]
        for v in range(H // 8):
            Z[pl.ds(g + 8 * v * G, 8, stride=G), :] = yre[8 * v:8 * v + 8]
            Z[pl.ds(g + (H + 8 * v) * G, 8, stride=G), :] = yim[8 * v:8 * v + 8]
        return 0

    lax.fori_loop(0, G, one, 0, unroll=max(1, min(G, 64 // S)))
    for k in range(S):
        src = me ^ k
        for cp in range(4):
            for j in range(JL):
                r = pl.multiple_of((cp * J + JL * src + j) * G, G)
                o_refs[k][cp // 2, cp % 2, :, 128 * j:128 * j + 128] = Z[pl.ds(r, G), :].astype(jnp.bfloat16)


def azimuth(me, taps, xs, begin, end):
    S = len(xs)
    rows = xs[0].shape[1]
    JL = rows // 4
    J = S * JL
    G = min(16, end - begin)
    skip = begin // G
    return pl.pallas_call(
        functools.partial(az_body, G, S, JL),
        grid=((end - begin) // G,),
        in_specs=[pl.BlockSpec(memory_space=pltpu.SMEM), pl.BlockSpec((G, 2, 2 * HALF, 128), lambda i: (i + skip, 0, 0, 0))]
        + [pl.BlockSpec((G, rows, 128), lambda i: (i + skip, 0, 0))] * S,
        out_specs=[pl.BlockSpec((2, 2, G, 128 * JL), lambda i: (0, 0, i, 0))] * S,
        out_shape=[jax.ShapeDtypeStruct((2, 2, end - begin, 128 * JL), jnp.bfloat16)] * S,
        scratch_shapes=[pltpu.VMEM((G, 4, J + 2 * HALF, 128), jnp.float32),
                        pltpu.VMEM((4 * J * G, 128), jnp.float32)],
        compiler_params=pltpu.CompilerParams(vmem_limit_bytes=24 * 2**20),
        cost_estimate=pl.CostEstimate(flops=int((end - begin) * 2.3e+07), bytes_accessed=32768 * (end - begin), transcendentals=0),
        name="azimuth",
    )(me, taps, *xs)


def assemble(me, groups, bins, pulses):
    pieces = [piece for _, _, group in groups for piece in group]
    total = len(pieces)

    def body(me_ref, *refs):
        spots, out, kept, loads, stores = refs[:total], refs[total], refs[total + 1:-2], refs[-2], refs[-1]
        reads, writes = [], []
        n = 0
        for first, stride, group in groups:
            for k in range(len(group)):
                width = group[k].shape[2]
                start = pl.multiple_of(first + (me_ref[0] ^ k) * stride, 16)
                reads.append(pltpu.make_async_copy(spots[n], kept[n], loads.at[n]))
                writes.append(pltpu.make_async_copy(kept[n], out.at[:, :, pl.ds(start, width), :], stores.at[n]))
                n += 1
        for copy in reads:
            copy.start()
        for read, write in zip(reads, writes):
            read.wait()
            write.start()
        for copy in writes:
            copy.wait()

    return pl.pallas_call(
        body,
        out_shape=jax.ShapeDtypeStruct((2, 2, bins, pulses), jnp.bfloat16),
        in_specs=[pl.BlockSpec(memory_space=pltpu.SMEM)] + [pl.BlockSpec(memory_space=pl.ANY)] * total,
        out_specs=pl.BlockSpec(memory_space=pl.ANY),
        scratch_shapes=[pltpu.VMEM(piece.shape, jnp.bfloat16) for piece in pieces]
        + [pltpu.SemaphoreType.DMA((total,))] * 2,
        compiler_params=pltpu.CompilerParams(vmem_limit_bytes=24 * 2**20),
        cost_estimate=pl.CostEstimate(flops=int(3.45e+09), bytes_accessed=0, transcendentals=0),
        name="assemble",
    )(me, *pieces)


def swap(pieces):
    peers = len(pieces)
    out = [pieces[0]]
    for k in range(1, peers):
        out.append(lax.ppermute(pieces[k], "pul", [(i, i ^ k) for i in range(peers)]))
    return out


def shards(raw, range_chirp, mig_weight, mig_offset, aperture, az_rate):
    bins = raw.shape[3]
    pulses = raw.shape[2]
    peers = lax.axis_size("pul")
    me = lax.axis_index("pul").astype(jnp.int32).reshape(1)
    blocks = bins // 128
    reach = range_chirp.shape[1] // 128 + (OFFMAX + BW) // 128
    half = blocks // 2
    own = 128 * half // peers
    near = raw[:, :, :, :128]
    echoes = raw
    far = echoes[:, :, :, 128:128 * reach]
    taps = []
    for n in range(2):
        begin = n * 128 * half + me[0] * own
        taps.append(taps_of(lax.dynamic_slice_in_dim(aperture, begin, own), lax.dynamic_slice_in_dim(az_rate, begin, own)))
    near = passed_along(near, "rng", -1)
    far = passed_along(far, "rng", -1)
    sources = [(raw, 0), (near, blocks), (far, blocks + 1)]
    first = swap(stage1(me, sources, range_chirp, mig_weight, mig_offset, 0, half, peers))
    second = swap(stage1(me, sources, range_chirp, mig_weight, mig_offset, half, half, peers))
    cut = max(own - 16 * LAST, 16)
    back0 = swap(azimuth(me, taps[0], first, 0, own))
    back1 = swap(azimuth(me, taps[1], second, 0, cut))
    groups = [(0, own, back0), (128 * half, own, back1)]
    if cut < own:
        tail, back0 = lax.optimization_barrier((taps[1], back0))
        groups[0] = (0, own, back0)
        last = list(azimuth(me, tail, second, cut, own))
        last[-1], back1[1] = lax.optimization_barrier((last[-1], back1[1]))
        groups.append((128 * half + cut, own, swap(last)))
    return assemble(me, groups, bins, pulses)


def solution(mesh):
    placed = (P(None, None, "pul", "rng"), P(), P(None, None, "rng"), P("rng"), P("rng"), P("rng"))
    return jax.shard_map(
        shards, mesh=mesh, in_specs=placed, out_specs=P(None, None, "rng", "pul"), check_vma=False
    )
```

```python
import functools
import math

import jax
import jax.numpy as jnp
from jax import lax
from jax.experimental import pallas as pl
from jax.experimental.pallas import tpu as pltpu
from jax.sharding import PartitionSpec as P

OFFMAX = 120
SPLIT = (2, 2)
LAST = 1


def turn(k, peers):
    return (peers - k) % peers


def passed_along(value, axis, by):
    peers = lax.axis_size(axis)
    pairs = [(i, i + by) for i in range(peers) if 0 <= i + by < peers]
    return lax.ppermute(value, axis, pairs)


BW = 8

def s1_body(first, count, peers, starts, me_ref, chirp_ref, w_ref, off_ref, *refs):
    n = len(starts)
    o_refs, Z, halos, sems = refs[n:n + peers], refs[n + peers], refs[n + peers + 1:-1], refs[-1]
    srcs = (refs[0],) + tuple(halos)
    arriving = {}
    for i in range(1, n):
        arriving[i] = pltpu.make_async_copy(refs[i], halos[i - 1], sems.at[i - 1])
        arriving[i].start()
    pulses = srcs[0].shape[2]
    tap_count = chirp_ref.shape[1]
    JL = pulses // 128
    span = tap_count // 128 + 1
    wide = 128 * span
    parts = []
    for c in range(2):
        row = chirp_ref[c:c + 1, :].astype(jnp.float32)
        row = jnp.concatenate([row, jnp.zeros((1, 128), jnp.float32)], axis=1)
        parts.append(pltpu.roll(jnp.broadcast_to(row, (128, wide)), 0, 1, stride=1, stride_axis=0))
    re, im = (v.astype(jnp.bfloat16) for v in parts)
    corr = jnp.concatenate([jnp.concatenate([re, im], axis=1), jnp.concatenate([-im, re], axis=1)], axis=0)

    def block(c, p, b):
        for i, (ref, start) in enumerate(zip(srcs, starts)):
            if start <= b < start + ref.shape[3] // 128:
                if i in arriving:
                    arriving.pop(i).wait()
                return ref[c, p, :, 128 * (b - start):128 * (b - start) + 128]

    def compressed(b):
        cols = []
        for p in range(2):
            win = jnp.concatenate([block(c, p, b + i) for c in range(2) for i in range(span)], axis=1)
            cols.append(lax.dot_general(corr, win, (((1,), (1,)), ((), ())), preferred_element_type=jnp.float32).astype(jnp.bfloat16))
        return jnp.concatenate(cols, axis=1)

    now = compressed(first)
    for q in range(count):
        nxt = compressed(first + q + 1)
        cols = [w_ref[0, :, 128 * q:128 * q + 128].astype(jnp.float32),
                w_ref[1, :, 128 * q:128 * q + 128].astype(jnp.float32),
                jnp.broadcast_to(off_ref[:, 128 * q:128 * q + 128].astype(jnp.float32), (8, 128)),
                jnp.zeros((128 - 3 * BW, 128), jnp.float32)]
        tab = jnp.concatenate(cols, axis=0).T
        lag = (lax.broadcasted_iota(jnp.int32, (128, 256), 1) - lax.broadcasted_iota(jnp.int32, (128, 256), 0)).astype(jnp.float32) - tab[:, 2 * BW:2 * BW + 1]
        wr = jnp.zeros((128, 256), jnp.float32)
        wi = jnp.zeros((128, 256), jnp.float32)
        for b in range(BW):
            hit = lag == float(b)
            wr = jnp.where(hit, tab[:, b:b + 1], wr)
            wi = jnp.where(hit, tab[:, BW + b:BW + b + 1], wi)
        wr = wr.astype(jnp.bfloat16)
        wi = wi.astype(jnp.bfloat16)
        top = jnp.concatenate([wr[:, :128], -wi[:, :128], wr[:, 128:], -wi[:, 128:]], axis=1)
        low = jnp.concatenate([wi[:, :128], wr[:, :128], wi[:, 128:], wr[:, 128:]], axis=1)
        lhs = jnp.concatenate([top, low], axis=0)
        rhs = jnp.concatenate([now, nxt], axis=0)
        y = jnp.dot(lhs, rhs, preferred_element_type=jnp.float32)
        R = 4 * JL
        for c in range(2):
            for p in range(2):
                for j in range(JL):
                    k = (2 * c + p) * JL + j
                    for t in range(16):
                        Z[pl.ds((128 * q + 8 * t) * R + k, 8, stride=R), :] = y[128 * c + 8 * t:128 * c + 8 * t + 8, (p * JL + j) * 128:(p * JL + j + 1) * 128]
        now = nxt
    own = 128 * count // peers
    for k in range(peers):
        start = pl.multiple_of((me_ref[0] ^ turn(k, peers)) * (own * R), own * R)
        o_refs[k][...] = Z[pl.ds(start, own * R), :].reshape(own, R, 128).astype(jnp.bfloat16)

def stage1(me, sources, chirp, weight, offset, first, count, peers):
    pulses = sources[0][0].shape[2]
    rows = 4 * pulses // 128
    own = 128 * count // peers
    last = first + count + chirp.shape[1] // 128
    specs, starts, values = [], [], []
    for value, start in sources:
        blocks = value.shape[3] // 128
        if start > last or start + blocks <= first:
            continue
        specs.append(pl.BlockSpec(memory_space=pl.ANY if values else pltpu.VMEM))
        starts.append(start)
        values.append(value)
    held = pl.BlockSpec(memory_space=pltpu.VMEM)
    w = weight[:, :, 128 * first:128 * (first + count)]
    off = offset.reshape(1, -1)[:, 128 * first:128 * (first + count)]
    return pl.pallas_call(
        functools.partial(s1_body, first, count, peers, tuple(starts)),
        out_shape=[jax.ShapeDtypeStruct((own, rows, 128), jnp.bfloat16)] * peers,
        in_specs=[pl.BlockSpec(memory_space=pltpu.SMEM)] + [held] * 3 + specs,
        out_specs=[held] * peers,
        scratch_shapes=[pltpu.VMEM((128 * count * rows, 128), jnp.float32)]
        + [pltpu.VMEM(value.shape, value.dtype) for value in values[1:]]
        + [pltpu.SemaphoreType.DMA((len(values) - 1,))],
        compiler_params=pltpu.CompilerParams(vmem_limit_bytes=24 * 2**20),
        cost_estimate=pl.CostEstimate(flops=int(1.38e+10 if first == 0 else 4.37e+09), bytes_accessed=4 << 20, transcendentals=0),
        name="range_stage",
    )(me, chirp, w, off, *values)


HALF = 4

def taps_of(aper, rate):
    n = aper.shape[0]
    shape = (n, 2 * HALF, 128)
    seg = lax.broadcasted_iota(jnp.int32, shape, 1)
    lane = lax.broadcasted_iota(jnp.int32, shape, 2)
    m = 128 * (seg - HALF) + ((128 - lane) & 127)
    aper = aper[:, None, None]; rate = rate[:, None, None]
    half_len = 64 * aper
    inside = (m >= -half_len) & (m < half_len)
    length = (128 * aper).astype(jnp.float32)
    mf = m.astype(jnp.float32)
    phase = math.pi * rate * (mf * mf) / length
    f = lax.rsqrt(length)
    re = jnp.where(inside, jnp.cos(phase) * f, 0.0)
    im = jnp.where(inside, -jnp.sin(phase) * f, 0.0)
    return jnp.stack([re, im], axis=1)


def az_body(G, S, JL, begin, end, me_ref, t_ref, *refs):
    x_refs, o_refs, (F, Z) = refs[:S], refs[S:2 * S], refs[2 * S:]
    me = me_ref[0]
    J = S * JL
    R = 4 * J
    H = R // 2
    NB = 2 * HALF + 1
    edge = jnp.zeros((G, 4, HALF, 128), jnp.float32)
    F[:, :, 0:HALF, :] = edge
    F[:, :, HALF + J:, :] = edge
    lower = lax.broadcasted_iota(jnp.int32, (128, 128), 0) >= lax.broadcasted_iota(jnp.int32, (128, 128), 1)

    def toeplitz(b, c):
        segs = t_ref[b, c]
        row = []
        for d in range(2 * HALF):
            wide = jnp.broadcast_to(segs[d:d + 1], (128, 128))
            row.append(pltpu.roll(wide, 0, 1, stride=1, stride_axis=0).astype(jnp.bfloat16))
        zero = jnp.zeros_like(row[0])
        row = [zero] + row + [zero]
        return [jnp.where(lower, row[d + 1], row[d]) for d in range(NB)]

    def group(n, _):
        base = pl.multiple_of(n * G, G)
        for k in range(S):
            src = me ^ turn(k, S)
            part = x_refs[k][pl.ds(begin + base, G)].astype(jnp.float32)
            for cp in range(4):
                F[:, cp, pl.ds(HALF + JL * src, JL), :] = part[:, JL * cp:JL * cp + JL]

        def one(g, _):
            lhs = [F[g, :, d:d + J, :].reshape(R, 128).astype(jnp.bfloat16) for d in range(NB)]
            re, im = toeplitz(begin + base + g, 0), toeplitz(begin + base + g, 1)
            rhs = jnp.concatenate([jnp.concatenate([re[d], im[d]], axis=1) for d in range(NB)], axis=0)
            y = jnp.dot(jnp.concatenate(lhs, axis=1), rhs, preferred_element_type=jnp.float32)
            yre = y[:H, :128] - y[H:, 128:]
            yim = y[:H, 128:] + y[H:, :128]
            for v in range(H // 8):
                Z[pl.ds(g + 8 * v * G, 8, stride=G), :] = yre[8 * v:8 * v + 8]
                Z[pl.ds(g + (H + 8 * v) * G, 8, stride=G), :] = yim[8 * v:8 * v + 8]
            return 0

        lax.fori_loop(0, G, one, 0, unroll=max(1, min(G, 64 // S)))
        for k in range(S):
            src = me ^ turn(k, S)
            for cp in range(4):
                for j in range(JL):
                    r = pl.multiple_of((cp * J + JL * src + j) * G, G)
                    o_refs[k][cp // 2, cp % 2, pl.ds(base, G), 128 * j:128 * j + 128] = Z[pl.ds(r, G), :].astype(jnp.bfloat16)
        return 0

    lax.fori_loop(0, (end - begin) // G, group, 0)


def azimuth(me, taps, xs, begin, end):
    S = len(xs)
    rows = xs[0].shape[1]
    JL = rows // 4
    J = S * JL
    G = min(16, end - begin)
    held = pl.BlockSpec(memory_space=pltpu.VMEM)
    return pl.pallas_call(
        functools.partial(az_body, G, S, JL, begin, end),
        in_specs=[pl.BlockSpec(memory_space=pltpu.SMEM)] + [held] * (S + 1),
        out_specs=[held] * S,
        out_shape=[jax.ShapeDtypeStruct((2, 2, end - begin, 128 * JL), jnp.bfloat16)] * S,
        scratch_shapes=[pltpu.VMEM((G, 4, J + 2 * HALF, 128), jnp.float32),
                        pltpu.VMEM((4 * J * G, 128), jnp.float32)],
        compiler_params=pltpu.CompilerParams(vmem_limit_bytes=24 * 2**20),
        cost_estimate=pl.CostEstimate(flops=int((end - begin) * 2.3e+07), bytes_accessed=32768 * (end - begin), transcendentals=0),
        name="azimuth",
    )(me, taps, *xs)


def assemble(me, groups, bins, pulses):
    pieces = [piece for _, _, group in groups for piece in group]
    total = len(pieces)

    def body(me_ref, *refs):
        spots, out, kept, loads, stores = refs[:total], refs[total], refs[total + 1:-2], refs[-2], refs[-1]
        reads, writes = [], []
        n = 0
        ready = len(groups[0][2])
        for first, stride, group in groups:
            for k in range(len(group)):
                width = group[k].shape[2]
                start = pl.multiple_of(first + (me_ref[0] ^ turn(k, len(group))) * stride, 16)
                held = spots[n] if n < ready else kept[n - ready]
                if n >= ready:
                    reads.append(pltpu.make_async_copy(spots[n], held, loads.at[n - ready]))
                writes.append(pltpu.make_async_copy(held, out.at[:, :, pl.ds(start, width), :], stores.at[n]))
                n += 1
        for copy in reads:
            copy.start()
        for copy in writes[:ready]:
            copy.start()
        for read, write in zip(reads, writes[ready:]):
            read.wait()
            write.start()
        for copy in writes:
            copy.wait()

    return pl.pallas_call(
        body,
        out_shape=jax.ShapeDtypeStruct((2, 2, bins, pulses), jnp.bfloat16),
        in_specs=[pl.BlockSpec(memory_space=pltpu.SMEM)] + [pl.BlockSpec(memory_space=pltpu.VMEM)] * len(groups[0][2])
        + [pl.BlockSpec(memory_space=pl.ANY)] * (total - len(groups[0][2])),
        out_specs=pl.BlockSpec(memory_space=pl.ANY),
        scratch_shapes=[pltpu.VMEM(piece.shape, jnp.bfloat16) for piece in pieces[len(groups[0][2]):]]
        + [pltpu.SemaphoreType.DMA((total - len(groups[0][2]),)), pltpu.SemaphoreType.DMA((total,))],
        compiler_params=pltpu.CompilerParams(vmem_limit_bytes=24 * 2**20),
        cost_estimate=pl.CostEstimate(flops=int(3.45e+09), bytes_accessed=0, transcendentals=0),
        name="assemble",
    )(me, *pieces)


def swap(pieces):
    peers = len(pieces)
    out = [pieces[0]]
    for k in range(1, peers):
        out.append(lax.ppermute(pieces[k], "pul", [(i, i ^ turn(k, peers)) for i in range(peers)]))
    return out


def shards(raw, range_chirp, mig_weight, mig_offset, aperture, az_rate):
    bins = raw.shape[3]
    pulses = raw.shape[2]
    peers = lax.axis_size("pul")
    me = lax.axis_index("pul").astype(jnp.int32).reshape(1)
    blocks = bins // 128
    reach = range_chirp.shape[1] // 128 + (OFFMAX + BW) // 128
    half = blocks // 2
    own = 128 * half // peers
    near = raw[:, :, :, :128]
    echoes = raw
    far = echoes[:, :, :, 128:128 * reach]
    taps = []
    for n in range(2):
        begin = n * 128 * half + me[0] * own
        taps.append(taps_of(lax.dynamic_slice_in_dim(aperture, begin, own), lax.dynamic_slice_in_dim(az_rate, begin, own)))
    near = passed_along(near, "rng", -1)
    far = passed_along(far, "rng", -1)
    sources = [(raw, 0), (near, blocks), (far, blocks + 1)]
    first = swap(stage1(me, sources, range_chirp, mig_weight, mig_offset, 0, half, peers))
    second = stage1(me, sources, range_chirp, mig_weight, mig_offset, half, half, peers)
    first[1], second = lax.optimization_barrier((first[1], second))
    second = swap(second)
    cut = max(own - 16 * LAST, 16)
    back0 = swap(azimuth(me, taps[0], first, 0, own))
    back1 = swap(azimuth(me, taps[1], second, 0, cut))
    groups = [(0, own, back0), (128 * half, own, back1)]
    if cut < own:
        tail, back0 = lax.optimization_barrier((taps[1], back0))
        groups[0] = (0, own, back0)
        last = list(azimuth(me, tail, second, cut, own))
        last[-1], back1[1] = lax.optimization_barrier((last[-1], back1[1]))
        groups.append((128 * half + cut, own, swap(last)))
    return assemble(me, groups, bins, pulses)


def solution(mesh):
    placed = (P(None, None, "pul", "rng"), P(), P(None, None, "rng"), P("rng"), P("rng"), P("rng"))
    return jax.shard_map(
        shards, mesh=mesh, in_specs=placed, out_specs=P(None, None, "rng", "pul"), check_vma=False
    )
```

```python
import functools
import math

import jax
import jax.numpy as jnp
from jax import lax
from jax.experimental import pallas as pl
from jax.experimental.pallas import tpu as pltpu
from jax.sharding import PartitionSpec as P

OFFMAX = 120
SPLIT = (2, 2)
LAST = 1


def turn(k, peers):
    return (peers - k) % peers


def passed_along(value, axis, by):
    peers = lax.axis_size(axis)
    pairs = [(i, i + by) for i in range(peers) if 0 <= i + by < peers]
    return lax.ppermute(value, axis, pairs)


BW = 8

def s1_body(first, count, peers, starts, me_ref, chirp_ref, w_ref, off_ref, *refs):
    n = len(starts)
    o_refs, Z, halos, sems = refs[n:n + peers], refs[n + peers], refs[n + peers + 1:-1], refs[-1]
    srcs = (refs[0],) + tuple(halos)
    arriving = {}
    for i in range(1, n):
        arriving[i] = pltpu.make_async_copy(refs[i], halos[i - 1], sems.at[i - 1])
        arriving[i].start()
    pulses = srcs[0].shape[2]
    tap_count = chirp_ref.shape[1]
    JL = pulses // 128
    span = tap_count // 128 + 1
    wide = 128 * span
    parts = []
    for c in range(2):
        row = chirp_ref[c:c + 1, :].astype(jnp.float32)
        row = jnp.concatenate([row, jnp.zeros((1, 128), jnp.float32)], axis=1)
        parts.append(pltpu.roll(jnp.broadcast_to(row, (128, wide)), 0, 1, stride=1, stride_axis=0))
    re, im = (v.astype(jnp.bfloat16) for v in parts)
    corr = jnp.concatenate([jnp.concatenate([re, im], axis=1), jnp.concatenate([-im, re], axis=1)], axis=0)

    def block(c, p, b):
        for i, (ref, start) in enumerate(zip(srcs, starts)):
            if start <= b < start + ref.shape[3] // 128:
                if i in arriving:
                    arriving.pop(i).wait()
                return ref[c, p, :, 128 * (b - start):128 * (b - start) + 128]

    def compressed(b):
        cols = []
        for p in range(2):
            win = jnp.concatenate([block(c, p, b + i) for c in range(2) for i in range(span)], axis=1)
            cols.append(lax.dot_general(corr, win, (((1,), (1,)), ((), ())), preferred_element_type=jnp.float32).astype(jnp.bfloat16))
        return jnp.concatenate(cols, axis=1)

    now = compressed(first)
    for q in range(count):
        nxt = compressed(first + q + 1)
        cols = [w_ref[0, :, 128 * q:128 * q + 128].astype(jnp.float32),
                w_ref[1, :, 128 * q:128 * q + 128].astype(jnp.float32),
                jnp.broadcast_to(off_ref[:, 128 * q:128 * q + 128].astype(jnp.float32), (8, 128)),
                jnp.zeros((128 - 3 * BW, 128), jnp.float32)]
        tab = jnp.concatenate(cols, axis=0).T
        lag = (lax.broadcasted_iota(jnp.int32, (128, 256), 1) - lax.broadcasted_iota(jnp.int32, (128, 256), 0)).astype(jnp.float32) - tab[:, 2 * BW:2 * BW + 1]
        wr = jnp.zeros((128, 256), jnp.float32)
        wi = jnp.zeros((128, 256), jnp.float32)
        for b in range(BW):
            hit = lag == float(b)
            wr = jnp.where(hit, tab[:, b:b + 1], wr)
            wi = jnp.where(hit, tab[:, BW + b:BW + b + 1], wi)
        wr = wr.astype(jnp.bfloat16)
        wi = wi.astype(jnp.bfloat16)
        top = jnp.concatenate([wr[:, :128], -wi[:, :128], wr[:, 128:], -wi[:, 128:]], axis=1)
        low = jnp.concatenate([wi[:, :128], wr[:, :128], wi[:, 128:], wr[:, 128:]], axis=1)
        lhs = jnp.concatenate([top, low], axis=0)
        rhs = jnp.concatenate([now, nxt], axis=0)
        y = jnp.dot(lhs, rhs, preferred_element_type=jnp.float32)
        R = 4 * JL
        for c in range(2):
            for p in range(2):
                for j in range(JL):
                    k = (2 * c + p) * JL + j
                    for t in range(16):
                        Z[pl.ds((128 * q + 8 * t) * R + k, 8, stride=R), :] = y[128 * c + 8 * t:128 * c + 8 * t + 8, (p * JL + j) * 128:(p * JL + j + 1) * 128]
        now = nxt
    own = 128 * count // peers
    for k in range(peers):
        start = pl.multiple_of((me_ref[0] ^ turn(k, peers)) * (own * R), own * R)
        o_refs[k][...] = Z[pl.ds(start, own * R), :].reshape(own, R, 128).astype(jnp.bfloat16)

def stage1(me, sources, chirp, weight, offset, first, count, peers):
    pulses = sources[0][0].shape[2]
    rows = 4 * pulses // 128
    own = 128 * count // peers
    last = first + count + chirp.shape[1] // 128
    specs, starts, values = [], [], []
    for value, start in sources:
        blocks = value.shape[3] // 128
        if start > last or start + blocks <= first:
            continue
        specs.append(pl.BlockSpec(memory_space=pl.ANY if values else pltpu.VMEM))
        starts.append(start)
        values.append(value)
    held = pl.BlockSpec(memory_space=pltpu.VMEM)
    w = weight[:, :, 128 * first:128 * (first + count)]
    off = offset.reshape(1, -1)[:, 128 * first:128 * (first + count)]
    return pl.pallas_call(
        functools.partial(s1_body, first, count, peers, tuple(starts)),
        out_shape=[jax.ShapeDtypeStruct((own, rows, 128), jnp.bfloat16)] * peers,
        in_specs=[pl.BlockSpec(memory_space=pltpu.SMEM)] + [held] * 3 + specs,
        out_specs=[held] * peers,
        scratch_shapes=[pltpu.VMEM((128 * count * rows, 128), jnp.float32)]
        + [pltpu.VMEM(value.shape, value.dtype) for value in values[1:]]
        + [pltpu.SemaphoreType.DMA((len(values) - 1,))],
        compiler_params=pltpu.CompilerParams(vmem_limit_bytes=24 * 2**20),
        cost_estimate=pl.CostEstimate(flops=int(1.38e+10 if first == 0 else 4.37e+09), bytes_accessed=4 << 20, transcendentals=0),
        name="range_stage",
    )(me, chirp, w, off, *values)


HALF = 4

def taps_of(aper, rate):
    n = aper.shape[0]
    shape = (n, 2 * HALF, 128)
    seg = lax.broadcasted_iota(jnp.int32, shape, 1)
    lane = lax.broadcasted_iota(jnp.int32, shape, 2)
    m = 128 * (seg - HALF) + ((128 - lane) & 127)
    aper = aper[:, None, None]; rate = rate[:, None, None]
    half_len = 64 * aper
    inside = (m >= -half_len) & (m < half_len)
    length = (128 * aper).astype(jnp.float32)
    mf = m.astype(jnp.float32)
    phase = math.pi * rate * (mf * mf) / length
    f = lax.rsqrt(length)
    re = jnp.where(inside, jnp.cos(phase) * f, 0.0)
    im = jnp.where(inside, -jnp.sin(phase) * f, 0.0)
    return jnp.stack([re, im], axis=1)


def az_body(G, S, JL, begin, end, me_ref, t_ref, *refs):
    x_refs, o_refs, (F, Z) = refs[:S], refs[S:2 * S], refs[2 * S:]
    me = me_ref[0]
    J = S * JL
    R = 4 * J
    H = R // 2
    NB = 2 * HALF + 1
    edge = jnp.zeros((G, 4, HALF, 128), jnp.float32)
    F[:, :, 0:HALF, :] = edge
    F[:, :, HALF + J:, :] = edge
    lower = lax.broadcasted_iota(jnp.int32, (128, 128), 0) >= lax.broadcasted_iota(jnp.int32, (128, 128), 1)

    def toeplitz(b, c):
        segs = t_ref[b, c]
        row = []
        for d in range(2 * HALF):
            wide = jnp.broadcast_to(segs[d:d + 1], (128, 128))
            row.append(pltpu.roll(wide, 0, 1, stride=1, stride_axis=0).astype(jnp.bfloat16))
        zero = jnp.zeros_like(row[0])
        row = [zero] + row + [zero]
        return [jnp.where(lower, row[d + 1], row[d]) for d in range(NB)]

    def group(n, _):
        base = pl.multiple_of(n * G, G)
        for k in range(S):
            src = me ^ turn(k, S)
            part = x_refs[k][pl.ds(begin + base, G)].astype(jnp.float32)
            for cp in range(4):
                F[:, cp, pl.ds(HALF + JL * src, JL), :] = part[:, JL * cp:JL * cp + JL]

        def one(g, _):
            lhs = [F[g, :, d:d + J, :].reshape(R, 128).astype(jnp.bfloat16) for d in range(NB)]
            re, im = toeplitz(begin + base + g, 0), toeplitz(begin + base + g, 1)
            rhs = jnp.concatenate([jnp.concatenate([re[d], im[d]], axis=1) for d in range(NB)], axis=0)
            y = jnp.dot(jnp.concatenate(lhs, axis=1), rhs, preferred_element_type=jnp.float32)
            yre = y[:H, :128] - y[H:, 128:]
            yim = y[:H, 128:] + y[H:, :128]
            for v in range(H // 8):
                Z[pl.ds(g + 8 * v * G, 8, stride=G), :] = yre[8 * v:8 * v + 8]
                Z[pl.ds(g + (H + 8 * v) * G, 8, stride=G), :] = yim[8 * v:8 * v + 8]
            return 0

        lax.fori_loop(0, G, one, 0, unroll=max(1, min(G, 64 // S)))
        for k in range(S):
            src = me ^ turn(k, S)
            for cp in range(4):
                for j in range(JL):
                    r = pl.multiple_of((cp * J + JL * src + j) * G, G)
                    o_refs[k][cp // 2, cp % 2, pl.ds(base, G), 128 * j:128 * j + 128] = Z[pl.ds(r, G), :].astype(jnp.bfloat16)
        return 0

    lax.fori_loop(0, (end - begin) // G, group, 0)


def azimuth(me, taps, xs, begin, end):
    S = len(xs)
    rows = xs[0].shape[1]
    JL = rows // 4
    J = S * JL
    G = min(16, end - begin)
    held = pl.BlockSpec(memory_space=pltpu.VMEM)
    return pl.pallas_call(
        functools.partial(az_body, G, S, JL, begin, end),
        in_specs=[pl.BlockSpec(memory_space=pltpu.SMEM)] + [held] * (S + 1),
        out_specs=[held] * S,
        out_shape=[jax.ShapeDtypeStruct((2, 2, end - begin, 128 * JL), jnp.bfloat16)] * S,
        scratch_shapes=[pltpu.VMEM((G, 4, J + 2 * HALF, 128), jnp.float32),
                        pltpu.VMEM((4 * J * G, 128), jnp.float32)],
        compiler_params=pltpu.CompilerParams(vmem_limit_bytes=24 * 2**20),
        cost_estimate=pl.CostEstimate(flops=int((end - begin) * 2.3e+07), bytes_accessed=32768 * (end - begin), transcendentals=0),
        name="azimuth",
    )(me, taps, *xs)


def assemble(me, groups, bins, pulses):
    pieces = [piece for _, _, group in groups for piece in group]
    total = len(pieces)

    def body(me_ref, *refs):
        spots, out, kept, loads, stores = refs[:total], refs[total], refs[total + 1:-2], refs[-2], refs[-1]
        reads, writes = [], []
        n = 0
        ready = len(pieces) - len(groups[-1][2])
        for first, stride, group in groups:
            for k in range(len(group)):
                width = group[k].shape[2]
                start = pl.multiple_of(first + (me_ref[0] ^ turn(k, len(group))) * stride, 16)
                held = spots[n] if n < ready else kept[n - ready]
                if n >= ready:
                    reads.append(pltpu.make_async_copy(spots[n], held, loads.at[n - ready]))
                writes.append(pltpu.make_async_copy(held, out.at[:, :, pl.ds(start, width), :], stores.at[n]))
                n += 1
        for copy in reads:
            copy.start()
        for copy in writes[:ready]:
            copy.start()
        for read, write in zip(reads, writes[ready:]):
            read.wait()
            write.start()
        for copy in writes:
            copy.wait()

    return pl.pallas_call(
        body,
        out_shape=jax.ShapeDtypeStruct((2, 2, bins, pulses), jnp.bfloat16),
        in_specs=[pl.BlockSpec(memory_space=pltpu.SMEM)] + [pl.BlockSpec(memory_space=pltpu.VMEM)] * (len(pieces) - len(groups[-1][2]))
        + [pl.BlockSpec(memory_space=pl.ANY)] * (total - (len(pieces) - len(groups[-1][2]))),
        out_specs=pl.BlockSpec(memory_space=pl.ANY),
        scratch_shapes=[pltpu.VMEM(piece.shape, jnp.bfloat16) for piece in pieces[len(pieces) - len(groups[-1][2]):]]
        + [pltpu.SemaphoreType.DMA((total - (len(pieces) - len(groups[-1][2])),)), pltpu.SemaphoreType.DMA((total,))],
        compiler_params=pltpu.CompilerParams(vmem_limit_bytes=24 * 2**20),
        cost_estimate=pl.CostEstimate(flops=int(3.45e+09), bytes_accessed=0, transcendentals=0),
        name="assemble",
    )(me, *pieces)


def swap(pieces):
    peers = len(pieces)
    out = [pieces[0]]
    for k in range(1, peers):
        out.append(lax.ppermute(pieces[k], "pul", [(i, i ^ turn(k, peers)) for i in range(peers)]))
    return out


def shards(raw, range_chirp, mig_weight, mig_offset, aperture, az_rate):
    bins = raw.shape[3]
    pulses = raw.shape[2]
    peers = lax.axis_size("pul")
    me = lax.axis_index("pul").astype(jnp.int32).reshape(1)
    blocks = bins // 128
    reach = range_chirp.shape[1] // 128 + (OFFMAX + BW) // 128
    half = blocks // 2
    own = 128 * half // peers
    near = raw[:, :, :, :128]
    echoes = raw
    far = echoes[:, :, :, 128:128 * reach]
    taps = []
    for n in range(2):
        begin = n * 128 * half + me[0] * own
        taps.append(taps_of(lax.dynamic_slice_in_dim(aperture, begin, own), lax.dynamic_slice_in_dim(az_rate, begin, own)))
    near = passed_along(near, "rng", -1)
    far = passed_along(far, "rng", -1)
    sources = [(raw, 0), (near, blocks), (far, blocks + 1)]
    first = swap(stage1(me, sources, range_chirp, mig_weight, mig_offset, 0, half, peers))
    second = stage1(me, sources, range_chirp, mig_weight, mig_offset, half, half, peers)
    first[1], second = lax.optimization_barrier((first[1], second))
    second = swap(second)
    cut = max(own - 16 * LAST, 16)
    back0 = swap(azimuth(me, taps[0], first, 0, own))
    back1 = swap(azimuth(me, taps[1], second, 0, cut))
    groups = [(0, own, back0), (128 * half, own, back1)]
    if cut < own:
        tail, back0 = lax.optimization_barrier((taps[1], back0))
        groups[0] = (0, own, back0)
        last = list(azimuth(me, tail, second, cut, own))
        last[-1], back1[1] = lax.optimization_barrier((last[-1], back1[1]))
        groups.append((128 * half + cut, own, swap(last)))
    return assemble(me, groups, bins, pulses)


def solution(mesh):
    placed = (P(None, None, "pul", "rng"), P(), P(None, None, "rng"), P("rng"), P("rng"), P("rng"))
    return jax.shard_map(
        shards, mesh=mesh, in_specs=placed, out_specs=P(None, None, "rng", "pul"), check_vma=False
    )
```
